32 devices in a mesh: res: 4 (over x, core), blk: 8 (over z, y).
Axes of the slice: x: 2, y: 2, z: 4, core: 2. Of those that a mesh axis runs over, the one named last changes fastest.
Arguments:
- modes: float32 [2, 8, 4194304], P(None, 'res', 'blk'), may hold values from -0.078125 to 0.078125
Outputs:
- product_modes: float32 [2, 8, 4194304], P(None, 'res', 'blk')
The draws below stay inside these ranges and needn't reach their ends.
All inputs are finite; a program needn't handle non-finite values.
Results may differ from the reference program's by a relative error of at most 0.000098.
Values sent between devices are 32-bit elements; how exact they have to be, the bound alone decides.
No kernel may reach another device: no remote copies, remote signals or barrier semaphores. Data moves between devices by JAX's collectives and lax.ppermute only.
A program may use at most 192 MiB of HBM per device.

```python
import jax
import jax.numpy as jnp

MODES = 33554432
EIGHTH = 4194304
PADDED = 50331648


def block_levels(key, extent, cuts, smallest, largest):
    gain, own = 1.0, jax.random.fold_in(key, 6)
    for dim, blocks in cuts:
        heights = jnp.exp(jax.random.uniform(jax.random.fold_in(own, dim), (blocks,), jnp.float32, smallest / len(cuts), largest / len(cuts)))
        gain = gain * jnp.repeat(heights, extent[dim] // blocks).reshape([-1 if axis == dim else 1 for axis in range(len(extent))])
    return gain


def gaussian(own_key, dims, scale, most, shards=(), dtype=jnp.bfloat16):
    loudness = block_levels(own_key, dims, shards, -0.22, 0.18) if shards else 1.0
    values = jax.random.normal(own_key, dims, jnp.float32) * scale * loudness
    return jnp.minimum(jnp.maximum(values, -most), most).astype(dtype)


def setup_inputs(seed: int = 0) -> dict:
    key_of = jax.random.split(jax.random.key(seed), 2)
    modes = gaussian(key_of[0], (2, 8, EIGHTH), (MODES ** -0.25), 0.078125, ((1, 4), (2, 8)), jnp.float32)
    return {"modes": modes}


def reference(modes):
    series = (modes[0] + 1j * modes[1]).reshape(MODES)
    padded = jnp.pad(series, (0, PADDED - MODES))
    physical = jnp.fft.ifft(padded) * PADDED
    spectrum = jnp.fft.fft(physical * physical) / PADDED
    kept = spectrum[MODES // 2: MODES // 2 + MODES]
    result = jnp.stack([jnp.real(kept), jnp.imag(kept)]).reshape(2, 8, EIGHTH)
    return result.astype(jnp.float32)
```

```python
import math

import jax
import jax.numpy as jnp
from jax import lax
from jax.sharding import PartitionSpec as P

AXES = ("res", "blk")
PARTS = 12
KEPT = 8
SKIP = 4

high = lax.Precision.HIGH


def iota(shape, axis):
    return lax.broadcasted_iota(jnp.int32, shape, axis)


def unit(position, period):
    angle = 2.0 * math.pi / period * (position % period).astype(jnp.float32)
    return jnp.cos(angle), jnp.sin(angle)


def cmul(left, right):
    return (
        left[0] * right[0] - left[1] * right[1],
        left[0] * right[1] + left[1] * right[0],
    )


def real_form(pair, sign, axes=(0, 2)):
    c, s = pair
    s = sign * s
    return jnp.stack([jnp.stack([c, -s], axes[1] - 1), jnp.stack([s, c], axes[1] - 1)], axes[0])


def on_device(modes):
    width = modes.shape[2]
    blocks = lax.axis_size("blk")
    groups = lax.axis_size("res")
    devices = blocks * groups
    own = KEPT // groups
    device = lax.axis_index("res") * blocks + lax.axis_index("blk")
    first = PARTS * blocks
    mine = first // devices
    padded = first * width
    chunk = width // devices
    inner = 512
    outer = width // inner
    share = chunk // inner if chunk >= inner else 1
    low = chunk // share

    order = (own, groups, blocks)
    place = (iota(order, 1) * own + iota(order, 0)) * blocks + iota(order, 2)
    place = place.reshape(1, KEPT * blocks)
    forward = real_form(unit(iota((first, 1), 0) * place, first), 1.0)
    backward = real_form(unit(iota((first, 1), 0) * (place + SKIP * blocks), first), -1.0)

    row_u = iota((first, share), 0)
    row = unit(row_u * (device * chunk + low * iota((first, share), 1)), padded)
    col = unit(iota((first, low), 0) * iota((first, low), 1), padded)
    turn = cmul((row[0][:, :, None], row[1][:, :, None]), (col[0][:, None], col[1][:, None]))

    got = lax.all_to_all(
        modes.reshape(2, own, devices, share, low), AXES, split_axis=2, concat_axis=2, tiled=True
    )
    got = got.reshape(2, KEPT * blocks, share, low)
    section = jnp.einsum("aubm,bmxc->auxc", forward, got, precision=high)
    section = jnp.stack(cmul(turn, section))
    back = lax.all_to_all(
        section.reshape(2, devices, mine, share, low), AXES, split_axis=1, concat_axis=1, tiled=True
    )
    local = back.reshape(2, devices, mine, chunk).transpose(0, 2, 1, 3).reshape(2, mine, outer, inner)

    outer_pair = unit(iota((outer, outer), 0) * iota((outer, outer), 1), outer)
    inner_pair = unit(iota((inner, inner), 0) * iota((inner, inner), 1), inner)
    inner_turn = unit(iota((outer, inner), 0) * iota((outer, inner), 1), width)

    local = jnp.einsum("asbp,bxpc->axsc", real_form(outer_pair, 1.0), local, precision=high)
    local = jnp.stack(cmul(inner_turn, local))
    values = jnp.einsum("akbj,bxsj->axsk", real_form(inner_pair, 1.0), local, precision=high)
    squared = jnp.stack(
        [(values[0] - values[1]) * (values[0] + values[1]), 2.0 * values[0] * values[1]]
    )
    local = jnp.einsum("akbj,bxsj->axsk", real_form(inner_pair, -1.0), squared, precision=high)
    local = jnp.stack(cmul((inner_turn[0], -inner_turn[1]), local))
    local = jnp.einsum("asbp,bxpc->axsc", real_form(outer_pair, -1.0), local, precision=high)

    moved = lax.all_to_all(
        local.reshape(2, mine, devices, share, low).transpose(0, 2, 1, 3, 4),
        AXES, split_axis=1, concat_axis=1, tiled=True,
    )
    moved = moved.reshape(2, first, share, low)
    moved = jnp.stack(cmul((turn[0] * (1.0 / padded), turn[1] * (-1.0 / padded)), moved))
    result = jnp.einsum(
        "aubm,buxc->amxc", backward, moved, precision=high
    )
    home = lax.all_to_all(
        result.reshape(2, own, devices, share, low), AXES, split_axis=2, concat_axis=2, tiled=True
    )
    return home.reshape(2, own, width)


def solution(mesh):
    return jax.shard_map(
        on_device,
        mesh=mesh,
        in_specs=(P(None, "res", "blk"),),
        out_specs=P(None, "res", "blk"),
        check_vma=False,
    )
```
